32 devices in a mesh: groups: 2 (over y), gx: 4 (over z), gy: 2 (over x), gz: 2 (over core).
Axes of the slice: x: 2, y: 2, z: 4, core: 2. Of those that a mesh axis runs over, the one named last changes fastest.
Arguments:
- log_perm: float32 [32, 32, 1024], P(('groups', 'gx'), 'gy', 'gz'), parts along dimension 0, may hold values from -4 to 4
- source: float32 [32, 32, 1024], P(('groups', 'gx'), 'gy', 'gz'), parts along dimension 0, may hold values from -24 to 24
- low_bound: float32 [1], replicated, may hold values from 0.05 to 0.4
- high_bound: float32 [1], replicated, may hold values from 1.8 to 2.4
Outputs:
- fine_pressure: float32 [32, 32, 1024], P(('groups', 'gx'), 'gy', 'gz'), parts along dimension 0
- difference: float32 [32, 32, 1024], P(('groups', 'gx'), 'gy', 'gz'), parts along dimension 0
The draws below stay inside these ranges and needn't reach their ends.
There are 2 independent parts, one for each index of `groups`. The reference program is written for one: setup_inputs(seed, part) draws one part's arguments, and reference() takes and returns one part's arrays. A program takes and returns all parts, laid end to end along the dimension named above; an argument that names none is the same for every part. Nothing has to cross between parts.
All inputs are finite; a program needn't handle non-finite values.
Results may differ from the reference program's by a relative error of at most 0.00002.
Values sent between devices are 32-bit elements; how exact they have to be, the bound alone decides.
A program may use at most 64 MiB of HBM per device.

```python
import jax
import jax.numpy as jnp

DEGREE = 3
NX = 16
NY = 32
NZ = 1024


def steps_of(own_key, dims, split, low, largest):
    factor_of, own = 1.0, jax.random.fold_in(own_key, 6)
    for position, shards_of in split:
        heights = jnp.exp(jax.random.uniform(jax.random.fold_in(own, position), (shards_of,), jnp.float32, low / len(split), largest / len(split)))
        factor_of = factor_of * jnp.repeat(heights, dims[position] // shards_of).reshape([-1 if axis == position else 1 for axis in range(len(dims))])
    return factor_of


def bell_draw(rng, extent, scale, most, split=(), kind=jnp.bfloat16):
    drawn = jax.random.normal(rng, extent, jnp.float32) * scale
    if len(split) > 0:
        drawn = steps_of(rng, extent, split, -0.22, 0.18) * drawn
    return jnp.clip(drawn, min=-most, max=most).astype(kind)


def setup_inputs(seed: int = 0, part: int = 0) -> dict:
    key_list = jax.random.split(jax.random.key(seed), 5)
    own_keys = jax.random.split(jax.random.fold_in(key_list[4], part), 5)
    return {
        "log_perm": bell_draw(own_keys[0], (NX, NY, NZ), 1.0, 4.0, ((0, 4), (1, 2), (2, 2)), jnp.float32),
        "source": bell_draw(own_keys[1], (NX, NY, NZ), 4.0, 24.0, ((0, 4), (1, 2), (2, 2)), jnp.float32),
        "low_bound": jnp.clip(jax.random.uniform(key_list[2], (1,), jnp.float32, 0.05, 0.4), 0.05, 0.4),
        "high_bound": jnp.clip(jax.random.uniform(key_list[3], (1,), jnp.float32, 1.8, 2.4), 1.8, 2.4),
    }


storage_rate = 0.1


def harmonic(first_perm, second_perm, face_scale):
    return face_scale * 2.0 * first_perm * second_perm / (first_perm + second_perm)


def coefficients(padded, face_scale, storage):
    centre = padded[1:-1, 1:-1, 1:-1]
    east_face = harmonic(centre, padded[2:, 1:-1, 1:-1], face_scale)
    west_face = harmonic(centre, padded[:-2, 1:-1, 1:-1], face_scale)
    north_face = harmonic(centre, padded[1:-1, 2:, 1:-1], face_scale)
    south_face = harmonic(centre, padded[1:-1, :-2, 1:-1], face_scale)
    upper_face = harmonic(centre, padded[1:-1, 1:-1, 2:], face_scale)
    lower_face = harmonic(centre, padded[1:-1, 1:-1, :-2], face_scale)
    diagonal = storage + east_face + west_face + north_face + south_face + upper_face + lower_face
    return (east_face, west_face, north_face, south_face, upper_face, lower_face, diagonal)


def operate(padded, face_terms):
    east_face, west_face, north_face, south_face, upper_face, lower_face, diagonal = face_terms
    centre = padded[1:-1, 1:-1, 1:-1]
    beside = east_face * padded[2:, 1:-1, 1:-1] + west_face * padded[:-2, 1:-1, 1:-1]
    beside = beside + north_face * padded[1:-1, 2:, 1:-1] + south_face * padded[1:-1, :-2, 1:-1]
    beside = beside + upper_face * padded[1:-1, 1:-1, 2:] + lower_face * padded[1:-1, 1:-1, :-2]
    return diagonal * centre - beside


def solve_level(log_field, source_field, lower_edge, upper_edge, face_scale, storage):
    face_terms = coefficients(jnp.pad(jnp.exp(log_field), 1), face_scale, storage)
    diagonal = face_terms[6]
    centre_value = (upper_edge + lower_edge) * 0.5
    half_width = (upper_edge - lower_edge) * 0.5
    ratio_sigma = centre_value / half_width
    rho_now = 1.0 / ratio_sigma
    direction = source_field / (centre_value * diagonal)
    solution = direction
    residual = source_field
    for iteration in range(DEGREE):
        residual = residual - operate(jnp.pad(direction, 1), face_terms)
        rho_next = 1.0 / (2.0 * ratio_sigma - rho_now)
        direction = rho_next * rho_now * direction + (2.0 * rho_next / half_width) * residual / diagonal
        solution = solution + direction
        rho_now = rho_next
    return solution


def reference(log_perm, source, low_bound, high_bound):
    lower_edge = low_bound[0]
    upper_edge = high_bound[0]
    fine = solve_level(log_perm, source, lower_edge, upper_edge, 1.0, storage_rate)
    blocks = (NX // 2, 2, NY // 2, 2, NZ // 2, 2)
    coarse_log = log_perm.reshape(blocks).mean(axis=(1, 3, 5))
    coarse_source = source.reshape(blocks).sum(axis=(1, 3, 5))
    coarse = solve_level(coarse_log, coarse_source, lower_edge, upper_edge, 2.0, 8.0 * storage_rate)
    spread = jnp.broadcast_to(coarse[:, None, :, None, :, None], blocks).reshape(NX, NY, NZ)
    return fine, fine - spread
```

```python
import functools

import jax
import jax.numpy as jnp
from jax import lax
from jax.experimental import pallas as pl
from jax.experimental.pallas import tpu as pltpu
from jax.sharding import PartitionSpec as P

DEGREE = 3
STORAGE = 0.1
LANES = 128
ROWS = 8
MESH = pl.DeviceIdType.MESH
AXES = ("gx", "gy", "gz")


def roll(a, shift, axis):
    return pltpu.roll(a, shift % a.shape[axis], axis)


def iota(shape, axis):
    return lax.broadcasted_iota(jnp.int32, shape, axis)


def even(shape, axis):
    return iota(shape, axis) % 2 == 0


def pair_sum(a, axis):
    return a + jnp.where(even(a.shape, axis), roll(a, -1, axis), roll(a, 1, axis))


def pooled(a, b):
    return pair_sum(pair_sum(a + b, 0), 1)


def packed(a):
    rows, lanes = a.shape[0] // 2, a.shape[1] // 2
    a = jnp.where(even((a.shape[0], lanes), 1), a[:, :lanes], a[:, lanes:])
    return jnp.where(even((rows, lanes), 0), a[:rows], a[rows:])


def unpacked(a):
    for axis in (0, 1):
        is_even = even(a.shape, axis)
        first = jnp.where(is_even, a, roll(a, 1, axis))
        second = jnp.where(is_even, roll(a, -1, axis), a)
        a = jnp.concatenate([first, second], axis=axis)
    return a


def kernel(sizes, low_ref, high_ref, log_hbm, src_hbm, fine_hbm, diff_hbm,
           log_ref, src_ref, fine_ref, diff_ref,
           dirs, face_c, face_y, halo_x, halo_c, halo_y, halo_z,
           inv_k, t_x, t_y, t_z, b_x, b_y, b_z, inv_d, res, sol,
           io_sem, send_sem, recv_sem):
    nx, ny, nz = log_ref.shape
    nc = nx // 2
    nl = nx + nc
    me = {axis: lax.axis_index(axis) for axis in AXES}
    has = {axis: (me[axis] > 0, me[axis] < sizes[axis] - 1) for axis in AXES}

    log_in = pltpu.make_async_copy(log_hbm, log_ref, io_sem.at[0])
    src_in = pltpu.make_async_copy(src_hbm, src_ref, io_sem.at[1])
    log_in.start()
    src_in.start()

    for halo in (halo_x, halo_c, halo_y, halo_z):
        halo[...] = jnp.zeros_like(halo)

    barrier = pltpu.get_barrier_semaphore()
    count = 0
    for axis in AXES:
        for side, step in ((0, -1), (1, 1)):
            if sizes[axis] > 1:
                @pl.when(has[axis][side])
                def _():
                    pl.semaphore_signal(barrier, inc=1, device_id={axis: me[axis] + step},
                                        device_id_type=MESH)
            count = count + has[axis][side].astype(jnp.int32)
    pl.semaphore_wait(barrier, count)

    def faces(turn, kind):
        if kind == 0:
            if turn == 0:
                return "gx", (lambda s: log_hbm.at[s * (nx - 1)]), (lambda s: halo_x.at[turn, s])
            return "gx", (lambda s: dirs.at[turn, s * (nx - 1)]), (lambda s: halo_x.at[turn, s])
        if kind == 1:
            return "gx", (lambda s: face_c.at[turn, s]), (lambda s: halo_c.at[turn, s])
        if kind == 2:
            return "gy", (lambda s: face_y.at[turn, s]), (lambda s: halo_y.at[turn, s])

        def lanes_of(s):
            start = s * (nz - LANES)
            if not isinstance(start, int):
                start = pl.multiple_of(start, LANES)
            return dirs.at[turn, :, :, pl.ds(start, LANES)]

        return "gz", lanes_of, (lambda s: halo_z.at[turn, s])

    def each(turn, kind, outgoing, act):
        axis, source_of, target_of = faces(turn, kind)
        n, here = sizes[axis], me[axis]
        if n == 1:
            return
        if n == 2:
            act(pltpu.make_async_remote_copy(
                src_ref=source_of(1 - here), dst_ref=target_of(here),
                send_sem=send_sem.at[turn, kind, 0], recv_sem=recv_sem.at[turn, kind, 0],
                device_id={axis: 1 - here}, device_id_type=MESH))
            return
        for side, step in ((0, -1), (1, 1)):
            there = 1 - side if outgoing else side

            @pl.when(has[axis][side])
            def _():
                act(pltpu.make_async_remote_copy(
                    src_ref=source_of(side), dst_ref=target_of(there),
                    send_sem=send_sem.at[turn, kind, side],
                    recv_sem=recv_sem.at[turn, kind, there],
                    device_id={axis: here + step}, device_id_type=MESH))

    def start(turn, kind):
        each(turn, kind, True, lambda copy: copy.start())

    def arrive(turn, kind):
        each(turn, kind, False, lambda copy: copy.wait_recv())

    def drain(turn, kind):
        each(turn, kind, True, lambda copy: copy.wait_send())

    start(0, 0)
    log_in.wait()

    def put(turn, i, value):
        dirs[turn, i] = value
        face_y[turn, 0, i:i + 1, :] = value[0:1, :]
        face_y[turn, 1, i:i + 1, :] = value[ny - 1:ny, :]
        if i >= nx and (i == nx or i == nl - 1):
            pack = packed(value)
            if i == nx:
                face_c[turn, 0] = pack
            if i == nl - 1:
                face_c[turn, 1] = pack

    def level(i):
        return (1, 1.0, STORAGE) if i < nx else (2, 2.0, 8.0 * STORAGE)

    order = [nx, nl - 1] + list(range(nx + 1, nl - 1)) + [0, nx - 1] + list(range(1, nx - 1))
    order = list(dict.fromkeys(order))
    for i in order:
        if i < nx:
            put(0, i, log_ref[i])
        else:
            j = 2 * (i - nx)
            put(0, i, pooled(log_ref[j], log_ref[j + 1]) * 0.125)
        if i == order[min(1, nc - 1)]:
            start(0, 1)
    start(0, 2)
    start(0, 3)

    row = iota((ny, nz), 0)
    lane = iota((ny, nz), 1)
    for i in range(nl):
        inv_k[i] = jnp.exp(-dirs[0, i])
    for i in range(nl):
        k, scale, storage = level(i)
        own = inv_k[i]
        along_y = jnp.where(row < ny - k, 2.0 * scale / (own + roll(own, -k, 0)), 0.0)
        along_z = jnp.where(lane < nz - k, 2.0 * scale / (own + roll(own, -k, 1)), 0.0)
        t_y[i] = along_y
        t_z[i] = along_z
        inv_d[i] = storage + (along_y + roll(along_y, k, 0)) + (along_z + roll(along_z, k, 1))
    for i in range(nl):
        if i not in (nx - 1, nl - 1):
            along_x = 2.0 * level(i)[1] / (inv_k[i] + inv_k[i + 1])
            t_x[i] = along_x
            inv_d[i] += along_x
            inv_d[i + 1] += along_x

    src_in.wait()
    for i in range(nl):
        if i < nx:
            res[i] = src_ref[i]
        else:
            j = 2 * (i - nx)
            res[i] = pooled(src_ref[j], src_ref[j + 1])

    low = jnp.full((1, nz), low_ref[0])
    high = jnp.full((1, nz), high_ref[0])
    theta = (high + low) * 0.5
    delta = (high - low) * 0.5
    sigma = theta / delta
    rho = 1.0 / sigma

    flag = {axis: tuple(h.astype(jnp.float32) for h in has[axis]) for axis in AXES}
    row_b = iota((ROWS, nz), 0)
    lane_b = iota((ny, LANES), 1)
    tile_y = (slice(0, ROWS), slice(ny - ROWS, ny))
    tile_z = (slice(0, LANES), slice(nz - LANES, nz))

    def side_x(turn, side, lev):
        return halo_x[turn, side] if lev == 0 else unpacked(halo_c[turn, side])

    def side_y(turn, side, i):
        return halo_y[turn, side, i:i + 1, :]

    def side_z(turn, side, i):
        k = level(i)[0]
        return roll(halo_z[turn, side, i], k if side == 0 else -k, 1)

    edge = {(0, 0): 0, (0, 1): nx - 1, (1, 0): nx, (1, 1): nl - 1}

    arrive(0, 3)
    for i in range(nl):
        k, scale, _ = level(i)
        for side in (0, 1):
            at = lane_b < k if side == 0 else lane_b >= LANES - k
            beyond = jnp.exp(-side_z(0, side, i))
            t = jnp.where(at, 2.0 * scale / (inv_k[i, :, tile_z[side]] + beyond), 0.0)
            t = t * flag["gz"][side]
            b_z[side, i] = t
            inv_d[i, :, tile_z[side]] += t
    arrive(0, 2)
    for i in range(nl):
        k, scale, _ = level(i)
        for side in (0, 1):
            at = row_b < k if side == 0 else row_b >= ROWS - k
            beyond = jnp.exp(-side_y(0, side, i))
            t = jnp.where(at, 2.0 * scale / (inv_k[i, tile_y[side], :] + beyond), 0.0)
            t = t * flag["gy"][side]
            b_y[side, i] = t
            inv_d[i, tile_y[side], :] += t
    arrive(0, 1)
    arrive(0, 0)
    for (lev, side), i in edge.items():
        t = 2.0 * level(i)[1] / (inv_k[i] + jnp.exp(-side_x(0, side, lev))) * flag["gx"][side]
        b_x[lev, side] = t
        inv_d[i] += t

    inv_theta = 1.0 / theta
    for i in order:
        inverse = 1.0 / inv_d[i]
        inv_d[i] = inverse
        direction = res[i] * inverse * inv_theta
        put(1, i, direction)
        sol[i] = direction
    for turn in range(1, DEGREE + 1):
        for kind in (0, 1, 2, 3):
            start(turn, kind)
        for i in range(nl):
            k, _, storage = level(i)
            d = dirs[turn, i]
            flow_y = t_y[i] * (d - roll(d, -k, 0))
            flow_z = t_z[i] * (d - roll(d, -k, 1))
            r = res[i] - storage * d
            r = r - (flow_y - roll(flow_y, k, 0)) - (flow_z - roll(flow_z, k, 1))
            if i not in (0, nx):
                r = r + t_x[i - 1] * (dirs[turn, i - 1] - d)
            if i not in (nx - 1, nl - 1):
                r = r - t_x[i] * (d - dirs[turn, i + 1])
            res[i] = r
        arrive(turn, 3)
        for i in range(nl):
            for side in (0, 1):
                at = tile_z[side]
                res[i, :, at] -= b_z[side, i] * (dirs[turn, i, :, at] - side_z(turn, side, i))
        arrive(turn, 2)
        for i in range(nl):
            for side in (0, 1):
                at = tile_y[side]
                res[i, at, :] -= b_y[side, i] * (dirs[turn, i, at, :] - side_y(turn, side, i))
        arrive(turn, 1)
        arrive(turn, 0)
        for (lev, side), i in edge.items():
            res[i] -= b_x[lev, side] * (dirs[turn, i] - side_x(turn, side, lev))
        rho_next = 1.0 / (2.0 * sigma - rho)
        keep = rho_next * rho
        gain = 2.0 * rho_next / delta
        rho = rho_next
        for i in order:
            direction = keep * dirs[turn, i] + gain * (res[i] * inv_d[i])
            if turn < DEGREE:
                sol[i] += direction
                put(turn + 1, i, direction)
            elif i >= nx:
                sol[i] += direction
            else:
                total = sol[i] + direction
                fine_ref[i] = total
                diff_ref[i] = total - sol[nx + i // 2]

    fine_out = pltpu.make_async_copy(fine_ref, fine_hbm, io_sem.at[2])
    diff_out = pltpu.make_async_copy(diff_ref, diff_hbm, io_sem.at[3])
    fine_out.start()
    diff_out.start()
    for turn in range(DEGREE + 1):
        for kind in (0, 1, 2, 3):
            drain(turn, kind)
    fine_out.wait()
    diff_out.wait()


def shards(sizes, log_perm, source, low_bound, high_bound):
    nx, ny, nz = log_perm.shape
    nc = nx // 2
    nl = nx + nc
    pack = -(-nl // ROWS) * ROWS
    turns = DEGREE + 1
    f32 = lambda *shape: pltpu.VMEM(shape, jnp.float32)
    block = f32(nx, ny, nz)
    both = f32(nl, ny, nz)
    shape = jax.ShapeDtypeStruct((nx, ny, nz), jnp.float32)
    smem = pl.BlockSpec(memory_space=pltpu.SMEM)
    hbm = pl.BlockSpec(memory_space=pl.ANY)
    return pl.pallas_call(
        functools.partial(kernel, sizes),
        out_shape=(shape, shape),
        in_specs=[smem, smem, hbm, hbm],
        out_specs=(hbm, hbm),
        scratch_shapes=[
            block, block, block, block,
            f32(turns, nl, ny, nz),
            f32(turns, 2, ny // 2, nz // 2),
            f32(turns, 2, pack, nz),
            f32(turns, 2, ny, nz),
            f32(turns, 2, ny // 2, nz // 2),
            f32(turns, 2, pack, nz),
            f32(turns, 2, nl, ny, LANES),
            both, both, both, both,
            f32(2, 2, ny, nz),
            f32(2, nl, ROWS, nz),
            f32(2, nl, ny, LANES),
            both, both, both,
            pltpu.SemaphoreType.DMA((4,)),
            pltpu.SemaphoreType.DMA((turns, 4, 2)),
            pltpu.SemaphoreType.DMA((turns, 4, 2)),
        ],
        compiler_params=pltpu.CompilerParams(collective_id=0, has_side_effects=True),
    )(low_bound, high_bound, log_perm, source)


def solution(mesh):
    sizes = {axis: mesh.shape[axis] for axis in AXES}
    spec = P(("groups", "gx"), "gy", "gz")
    return jax.shard_map(
        functools.partial(shards, sizes),
        mesh=mesh,
        in_specs=(spec, spec, P(), P()),
        out_specs=(spec, spec),
        check_vma=False,
    )
```

```python
import functools

import jax
import jax.numpy as jnp
from jax import lax
from jax.experimental import pallas as pl
from jax.experimental.pallas import tpu as pltpu
from jax.sharding import PartitionSpec as P

DEGREE = 3
STORAGE = 0.1
LANES = 128
ROWS = 8
MESH = pl.DeviceIdType.MESH
AXES = ("gx", "gy", "gz")


def roll(a, shift, axis):
    return pltpu.roll(a, shift % a.shape[axis], axis)


def iota(shape, axis):
    return lax.broadcasted_iota(jnp.int32, shape, axis)


def even(shape, axis):
    return iota(shape, axis) % 2 == 0


def pair_sum(a, axis):
    return a + jnp.where(even(a.shape, axis), roll(a, -1, axis), roll(a, 1, axis))


def pooled(a, b):
    return pair_sum(pair_sum(a + b, 0), 1)


def packed(a):
    rows, lanes = a.shape[0] // 2, a.shape[1] // 2
    a = jnp.where(even((a.shape[0], lanes), 1), a[:, :lanes], a[:, lanes:])
    return jnp.where(even((rows, lanes), 0), a[:rows], a[rows:])


def unpacked(a):
    for axis in (0, 1):
        is_even = even(a.shape, axis)
        first = jnp.where(is_even, a, roll(a, 1, axis))
        second = jnp.where(is_even, roll(a, -1, axis), a)
        a = jnp.concatenate([first, second], axis=axis)
    return a


def kernel(sizes, low_ref, high_ref, log_hbm, src_hbm, sol, last,
           log_ref, src_ref, dirs, face_c, face_y, halo_x, halo_c, halo_y, halo_z,
           inv_k, t_x, t_y, t_z, b_x, b_y, b_z, held, inv_d, res,
           io_sem, send_sem, recv_sem):
    nx, ny, nz = log_ref.shape
    nc = nx // 2
    nl = nx + nc
    me = {axis: lax.axis_index(axis) for axis in AXES}
    has = {axis: (me[axis] > 0, me[axis] < sizes[axis] - 1) for axis in AXES}

    log_in = pltpu.make_async_copy(log_hbm, log_ref, io_sem.at[0])
    src_in = pltpu.make_async_copy(src_hbm, src_ref, io_sem.at[1])
    log_in.start()
    src_in.start()

    for axis, halos in (("gx", (halo_x, halo_c)), ("gy", (halo_y,)), ("gz", (halo_z,))):
        if sizes[axis] > 2:
            for halo in halos:
                halo[...] = jnp.zeros_like(halo)

    barrier = pltpu.get_barrier_semaphore()
    count = 0
    for axis in AXES:
        for side, step in ((0, -1), (1, 1)):
            if sizes[axis] > 1:
                @pl.when(has[axis][side])
                def _():
                    pl.semaphore_signal(barrier, inc=1, device_id={axis: me[axis] + step},
                                        device_id_type=MESH)
            count = count + has[axis][side].astype(jnp.int32)

    def sides(axis):
        if sizes[axis] == 1:
            return []
        if sizes[axis] == 2:
            return [(0, 1 - me[axis], None)]
        return [(s, s, has[axis][s].astype(jnp.float32)) for s in (0, 1)]

    def tile(side, length, size):
        first = side * (length - size)
        return pl.ds(first if isinstance(first, int) else pl.multiple_of(first, size), size)

    def faces(turn, kind):
        if kind == 0:
            source = log_hbm if turn == 0 else dirs.at[turn]
            return "gx", (lambda s: source.at[s * (nx - 1)]), (lambda s: halo_x.at[turn, s])
        if kind == 1:
            return "gx", (lambda s: face_c.at[turn, s]), (lambda s: halo_c.at[turn, s])
        if kind == 2:
            return "gy", (lambda s: face_y.at[turn, s]), (lambda s: halo_y.at[turn, s])
        return ("gz", (lambda s: dirs.at[turn, :, :, tile(s, nz, LANES)]),
                (lambda s: halo_z.at[turn, s]))

    def each(turn, kind, outgoing, act):
        axis, source_of, target_of = faces(turn, kind)
        n, here = sizes[axis], me[axis]
        if n == 1:
            return
        if n == 2:
            act(pltpu.make_async_remote_copy(
                src_ref=source_of(1 - here), dst_ref=target_of(here),
                send_sem=send_sem.at[turn, kind, 0], recv_sem=recv_sem.at[turn, kind, 0],
                device_id={axis: 1 - here}, device_id_type=MESH))
            return
        for side, step in ((0, -1), (1, 1)):
            there = 1 - side if outgoing else side

            @pl.when(has[axis][side])
            def _():
                act(pltpu.make_async_remote_copy(
                    src_ref=source_of(side), dst_ref=target_of(there),
                    send_sem=send_sem.at[turn, kind, side],
                    recv_sem=recv_sem.at[turn, kind, there],
                    device_id={axis: here + step}, device_id_type=MESH))

    def start(turn, kind):
        each(turn, kind, True, lambda copy: copy.start())

    def arrive(turn, kind):
        each(turn, kind, False, lambda copy: copy.wait_recv())

    def drain(turn, kind):
        each(turn, kind, True, lambda copy: copy.wait_send())

    def field(turn):
        return dirs.at[turn] if turn <= DEGREE else last

    def level(i):
        return (1, 1.0, STORAGE) if i < nx else (2, 2.0, 8.0 * STORAGE)

    def send_coarse(turn):
        face_c[turn, 0] = packed(dirs[turn, nx])
        face_c[turn, 1] = packed(dirs[turn, nl - 1])
        start(turn, 1)

    def send_rows(turn):
        for i in range(nl):
            face_y[turn, 0, i:i + 1, :] = dirs[turn, i, 0:1, :]
            face_y[turn, 1, i:i + 1, :] = dirs[turn, i, ny - 1:ny, :]
        start(turn, 2)

    log_in.wait()
    for i in range(nx):
        dirs[0, i] = log_ref[i]
    for j in range(nc):
        dirs[0, nx + j] = pooled(log_ref[2 * j], log_ref[2 * j + 1]) * 0.125
    pl.semaphore_wait(barrier, count)
    start(0, 0)
    send_coarse(0)
    send_rows(0)
    start(0, 3)

    row = iota((ny, nz), 0)
    lane = iota((ny, nz), 1)
    for i in range(nl):
        inv_k[i] = jnp.exp(-dirs[0, i])
    for i in range(nl):
        k, scale, storage = level(i)
        own = inv_k[i]
        along_y = jnp.where(row < ny - k, 2.0 * scale / (own + roll(own, -k, 0)), 0.0)
        along_z = jnp.where(lane < nz - k, 2.0 * scale / (own + roll(own, -k, 1)), 0.0)
        t_y[i] = along_y
        t_z[i] = along_z
        inv_d[i] = (along_y + roll(along_y, k, 0)) + (along_z + roll(along_z, k, 1))
        held[i] = jnp.full((ny, nz), storage)
    for i in range(nl):
        if i not in (nx - 1, nl - 1):
            along_x = 2.0 * level(i)[1] / (inv_k[i] + inv_k[i + 1])
            t_x[i] = along_x
            inv_d[i] += along_x
            inv_d[i + 1] += along_x

    src_in.wait()
    for i in range(nx):
        res[i] = src_ref[i]
    for j in range(nc):
        res[nx + j] = pooled(src_ref[2 * j], src_ref[2 * j + 1])

    low = jnp.full((1, nz), low_ref[0])
    high = jnp.full((1, nz), high_ref[0])
    theta = (high + low) * 0.5
    delta = (high - low) * 0.5
    sigma = theta / delta
    rho = 1.0 / sigma
    inv_theta = 1.0 / theta

    row_b = iota((ROWS, nz), 0)
    lane_b = iota((ny, LANES), 1)

    def beside(index, side, size, k):
        first = side * (size - k)
        return (index >= first) & (index < first + k)

    def side_x(turn, side, lev):
        return halo_x[turn, side] if lev == 0 else unpacked(halo_c[turn, side])

    def side_y(turn, side, i):
        return halo_y[turn, side, i:i + 1, :]

    def side_z(turn, side, i):
        k = level(i)[0]
        return pltpu.roll(halo_z[turn, side, i], k + side * (LANES - 2 * k), 1)

    def edge(lev, side):
        if isinstance(side, int):
            return (0, nx - 1)[side] if lev == 0 else (nx, nl - 1)[side]
        return side * (nx - 1) if lev == 0 else nx + side * (nc - 1)

    def across(at, scale, own, beyond, factor):
        t = 2.0 * scale / (own + jnp.exp(-beyond))
        if at is not None:
            t = jnp.where(at, t, 0.0)
        return t if factor is None else t * factor

    arrive(0, 3)
    for slot, side, factor in sides("gz"):
        where = tile(side, nz, LANES)
        for i in range(nl):
            k, scale, _ = level(i)
            t = across(beside(lane_b, side, LANES, k), scale, inv_k[i, :, where],
                       side_z(0, side, i), factor)
            b_z[slot, i] = t
            held[i, :, where] += t
    arrive(0, 2)
    for slot, side, factor in sides("gy"):
        where = tile(side, ny, ROWS)
        for i in range(nl):
            k, scale, _ = level(i)
            t = across(beside(row_b, side, ROWS, k), scale, inv_k[i, where, :],
                       side_y(0, side, i), factor)
            b_y[slot, i] = t
            held[i, where, :] += t

    def begin(i):
        inverse = 1.0 / (inv_d[i] + held[i])
        inv_d[i] = inverse
        dirs[1, i] = res[i] * inverse * inv_theta

    for i in range(1, nx - 1):
        begin(i)
    for lev in (0, 1):
        arrive(0, lev)
        for slot, side, factor in sides("gx"):
            i = edge(lev, side)
            t = across(None, (1.0, 2.0)[lev], inv_k[i], side_x(0, side, lev), factor)
            b_x[lev, slot] = t
            held[i] += t
        if lev == 0:
            for i in dict.fromkeys((0, nx - 1)):
                begin(i)
            start(1, 0)
    for i in range(nx, nl):
        begin(i)
    send_coarse(1)
    send_rows(1)
    start(1, 3)

    for turn in range(1, DEGREE + 1):
        rho_next = 1.0 / (2.0 * sigma - rho)
        keep = rho_next * rho
        gain = 2.0 * rho_next / delta
        rho = rho_next
        later = field(turn + 1)
        flow_x = None
        for i in range(nl):
            k = level(i)[0]
            d = dirs[turn, i]
            sol[i] = d if turn == 1 else sol[i] + d
            flow_y = t_y[i] * (d - roll(d, -k, 0))
            flow_z = t_z[i] * (d - roll(d, -k, 1))
            r = res[i] - held[i] * d
            r = r - (flow_y - roll(flow_y, k, 0)) - (flow_z - roll(flow_z, k, 1))
            if i not in (0, nx):
                r = r + flow_x
            if i not in (nx - 1, nl - 1):
                flow_x = t_x[i] * (d - dirs[turn, i + 1])
                r = r - flow_x
            res[i] = r
            later[i] = keep * d + gain * (r * inv_d[i])

        def add(at, t, wide):
            if turn < DEGREE:
                res[at] += t
            later[at] += wide * (t * inv_d[at])

        arrive(turn, 3)
        for slot, side, _ in sides("gz"):
            for i in range(nl):
                add((i, slice(None), tile(side, nz, LANES)),
                    b_z[slot, i] * side_z(turn, side, i), gain[:, :LANES])
        arrive(turn, 2)
        for slot, side, _ in sides("gy"):
            for i in range(nl):
                add((i, tile(side, ny, ROWS), slice(None)),
                    b_y[slot, i] * side_y(turn, side, i), gain)
        for lev in (0, 1):
            arrive(turn, lev)
            for slot, side, _ in sides("gx"):
                add((edge(lev, side),), b_x[lev, slot] * side_x(turn, side, lev), gain)
            if lev == 0 and turn < DEGREE:
                start(turn + 1, 0)
        if turn < DEGREE:
            send_coarse(turn + 1)
            send_rows(turn + 1)
            start(turn + 1, 3)

    for turn in range(DEGREE + 1):
        for kind in (0, 1, 2, 3):
            drain(turn, kind)


def shards(sizes, log_perm, source, low_bound, high_bound):
    nx, ny, nz = log_perm.shape
    nc = nx // 2
    nl = nx + nc
    pack = -(-nl // ROWS) * ROWS
    turns = DEGREE + 1
    f32 = lambda *shape: pltpu.VMEM(shape, jnp.float32)
    block = f32(nx, ny, nz)
    both = f32(nl, ny, nz)
    shape = jax.ShapeDtypeStruct((nl, ny, nz), jnp.float32)
    smem = pl.BlockSpec(memory_space=pltpu.SMEM)
    hbm = pl.BlockSpec(memory_space=pl.ANY)
    vmem = pl.BlockSpec(memory_space=pltpu.VMEM)
    sol, last = pl.pallas_call(
        functools.partial(kernel, sizes),
        out_shape=(shape, shape),
        in_specs=[smem, smem, hbm, hbm],
        out_specs=(vmem, vmem),
        scratch_shapes=[
            block, block,
            f32(turns, nl, ny, nz),
            f32(turns, 2, ny // 2, nz // 2),
            f32(turns, 2, pack, nz),
            f32(turns, 2, ny, nz),
            f32(turns, 2, ny // 2, nz // 2),
            f32(turns, 2, pack, nz),
            f32(turns, 2, nl, ny, LANES),
            both, both, both, both,
            f32(2, 2, ny, nz),
            f32(2, nl, ROWS, nz),
            f32(2, nl, ny, LANES),
            both, both, both,
            pltpu.SemaphoreType.DMA((2,)),
            pltpu.SemaphoreType.DMA((turns, 4, 2)),
            pltpu.SemaphoreType.DMA((turns, 4, 2)),
        ],
        compiler_params=pltpu.CompilerParams(
            collective_id=0, has_side_effects=True, vmem_limit_bytes=16 * 2**20),
    )(low_bound, high_bound, log_perm, source)
    total = sol + last
    fine = total[:nx]
    return fine, fine - jnp.repeat(total[nx:], 2, axis=0)


def solution(mesh):
    sizes = {axis: mesh.shape[axis] for axis in AXES}
    spec = P(("groups", "gx"), "gy", "gz")
    return jax.shard_map(
        functools.partial(shards, sizes),
        mesh=mesh,
        in_specs=(spec, spec, P(), P()),
        out_specs=(spec, spec),
        check_vma=False,
    )
```

```python
import functools

import jax
import jax.numpy as jnp
from jax import lax
from jax.experimental import pallas as pl
from jax.experimental.pallas import tpu as pltpu
from jax.sharding import PartitionSpec as P

DEGREE = 3
STORAGE = 0.1
LANES = 128
ROWS = 8
MESH = pl.DeviceIdType.MESH
AXES = ("gx", "gy", "gz")


def roll(a, shift, axis):
    return pltpu.roll(a, shift % a.shape[axis], axis)


def iota(shape, axis):
    return lax.broadcasted_iota(jnp.int32, shape, axis)


def even(shape, axis):
    return iota(shape, axis) % 2 == 0


def pair_sum(a, axis):
    return a + jnp.where(even(a.shape, axis), roll(a, -1, axis), roll(a, 1, axis))


def pooled(a, b):
    return pair_sum(pair_sum(a + b, 0), 1)


def packed(a):
    rows, lanes = a.shape[0] // 2, a.shape[1] // 2
    a = jnp.where(even((a.shape[0], lanes), 1), a[:, :lanes], a[:, lanes:])
    return jnp.where(even((rows, lanes), 0), a[:rows], a[rows:])


def unpacked(a):
    for axis in (0, 1):
        is_even = even(a.shape, axis)
        first = jnp.where(is_even, a, roll(a, 1, axis))
        second = jnp.where(is_even, roll(a, -1, axis), a)
        a = jnp.concatenate([first, second], axis=axis)
    return a


def kernel(sizes, low_hbm, high_hbm, log_hbm, src_hbm, sol, last,
           low_ref, high_ref, log_ref, src_ref, dirs, face_c, face_y, halo_x, halo_c, halo_y, halo_z,
           inv_k, t_x, t_y, t_z, b_x, b_y, b_z, held, inv_d, res,
           io_sem, send_sem, recv_sem):
    nx, ny, nz = log_ref.shape
    nc = nx // 2
    nl = nx + nc
    me = {axis: lax.axis_index(axis) for axis in AXES}
    has = {axis: (me[axis] > 0, me[axis] < sizes[axis] - 1) for axis in AXES}

    barrier = pltpu.get_barrier_semaphore()
    count = 0
    for axis in AXES:
        if sizes[axis] == 2:
            pl.semaphore_signal(barrier, inc=1, device_id={axis: 1 - me[axis]},
                                device_id_type=MESH)
            count = count + 1
        elif sizes[axis] > 2:
            for side, step in ((0, -1), (1, 1)):
                @pl.when(has[axis][side])
                def _():
                    pl.semaphore_signal(barrier, inc=1, device_id={axis: me[axis] + step},
                                        device_id_type=MESH)
                count = count + has[axis][side].astype(jnp.int32)

    log_in = pltpu.make_async_copy(log_hbm, log_ref, io_sem.at[0])
    src_in = pltpu.make_async_copy(src_hbm, src_ref, io_sem.at[1])
    low_in = pltpu.make_async_copy(low_hbm, low_ref, io_sem.at[2])
    high_in = pltpu.make_async_copy(high_hbm, high_ref, io_sem.at[3])
    for copy in (log_in, src_in, low_in, high_in):
        copy.start()

    for axis, halos in (("gx", (halo_x, halo_c)), ("gy", (halo_y,)), ("gz", (halo_z,))):
        if sizes[axis] > 2:
            for side in (0, 1):
                @pl.when(jnp.logical_not(has[axis][side]))
                def _():
                    for halo in halos:
                        for turn in range(DEGREE + 1):
                            halo[turn, side] = jnp.zeros_like(halo[turn, side])

    def sides(axis):
        if sizes[axis] == 1:
            return []
        if sizes[axis] == 2:
            return [(0, 1 - me[axis], None)]
        return [(s, s, has[axis][s].astype(jnp.float32)) for s in (0, 1)]

    def tile(side, length, size):
        first = side * (length - size)
        return pl.ds(first if isinstance(first, int) else pl.multiple_of(first, size), size)

    def faces(turn, kind):
        if kind == 0:
            source = log_hbm if turn == 0 else dirs.at[turn]
            return "gx", (lambda s: source.at[s * (nx - 1)]), (lambda s: halo_x.at[turn, s])
        if kind == 1:
            return "gx", (lambda s: face_c.at[turn, s]), (lambda s: halo_c.at[turn, s])
        if kind == 2:
            return "gy", (lambda s: face_y.at[turn, s]), (lambda s: halo_y.at[turn, s])
        return ("gz", (lambda s: dirs.at[turn, :, :, tile(s, nz, LANES)]),
                (lambda s: halo_z.at[turn, s]))

    def each(turn, kind, outgoing, act):
        axis, source_of, target_of = faces(turn, kind)
        n, here = sizes[axis], me[axis]
        if n == 1:
            return
        if n == 2:
            act(pltpu.make_async_remote_copy(
                src_ref=source_of(1 - here), dst_ref=target_of(here),
                send_sem=send_sem.at[turn, kind, 0], recv_sem=recv_sem.at[turn, kind, 0],
                device_id={axis: 1 - here}, device_id_type=MESH))
            return
        for side, step in ((0, -1), (1, 1)):
            there = 1 - side if outgoing else side

            @pl.when(has[axis][side])
            def _():
                act(pltpu.make_async_remote_copy(
                    src_ref=source_of(side), dst_ref=target_of(there),
                    send_sem=send_sem.at[turn, kind, side],
                    recv_sem=recv_sem.at[turn, kind, there],
                    device_id={axis: here + step}, device_id_type=MESH))

    def start(turn, kind):
        each(turn, kind, True, lambda copy: copy.start())

    def arrive(turn, kind):
        each(turn, kind, False, lambda copy: copy.wait_recv())

    def drain(turn, kind):
        each(turn, kind, True, lambda copy: copy.wait_send())

    def field(turn):
        return dirs.at[turn] if turn <= DEGREE else last

    def level(i):
        return (1, 1.0, STORAGE) if i < nx else (2, 2.0, 8.0 * STORAGE)

    def send_coarse(turn):
        face_c[turn, 0] = packed(dirs[turn, nx])
        face_c[turn, 1] = packed(dirs[turn, nl - 1])
        start(turn, 1)

    def send_rows(turn):
        for i in range(nl):
            face_y[turn, 0, i:i + 1, :] = dirs[turn, i, 0:1, :]
            face_y[turn, 1, i:i + 1, :] = dirs[turn, i, ny - 1:ny, :]
        start(turn, 2)

    log_in.wait()
    for i in range(nx):
        dirs[0, i] = log_ref[i]
    for j in range(nc):
        dirs[0, nx + j] = pooled(log_ref[2 * j], log_ref[2 * j + 1]) * 0.125
    pl.semaphore_wait(barrier, count)
    start(0, 0)
    send_coarse(0)
    send_rows(0)
    start(0, 3)

    row = iota((ny, nz), 0)
    lane = iota((ny, nz), 1)
    for i in range(nl):
        inv_k[i] = jnp.exp(-dirs[0, i])
    for i in range(nl):
        k, scale, storage = level(i)
        own = inv_k[i]
        along_y = jnp.where(row < ny - k, 2.0 * scale / (own + roll(own, -k, 0)), 0.0)
        along_z = jnp.where(lane < nz - k, 2.0 * scale / (own + roll(own, -k, 1)), 0.0)
        t_y[i] = along_y
        t_z[i] = along_z
        inv_d[i] = (along_y + roll(along_y, k, 0)) + (along_z + roll(along_z, k, 1))
        held[i] = jnp.full((ny, nz), storage)
    for i in range(nl):
        if i not in (nx - 1, nl - 1):
            along_x = 2.0 * level(i)[1] / (inv_k[i] + inv_k[i + 1])
            t_x[i] = along_x
            inv_d[i] += along_x
            inv_d[i + 1] += along_x

    for copy in (src_in, low_in, high_in):
        copy.wait()
    for i in range(nx):
        res[i] = src_ref[i]
    for j in range(nc):
        res[nx + j] = pooled(src_ref[2 * j], src_ref[2 * j + 1])

    low = jnp.full((1, nz), low_ref[0])
    high = jnp.full((1, nz), high_ref[0])
    theta = (high + low) * 0.5
    delta = (high - low) * 0.5
    sigma = theta / delta
    rho = 1.0 / sigma
    inv_theta = 1.0 / theta

    row_b = iota((ROWS, nz), 0)
    lane_b = iota((ny, LANES), 1)

    def beside(index, side, size, k):
        first = side * (size - k)
        return (index >= first) & (index < first + k)

    def side_x(turn, side, lev):
        return halo_x[turn, side] if lev == 0 else unpacked(halo_c[turn, side])

    def side_y(turn, side, i):
        return halo_y[turn, side, i:i + 1, :]

    def side_z(turn, side, i):
        k = level(i)[0]
        return pltpu.roll(halo_z[turn, side, i], k + side * (LANES - 2 * k), 1)

    def edge(lev, side):
        if isinstance(side, int):
            return (0, nx - 1)[side] if lev == 0 else (nx, nl - 1)[side]
        return side * (nx - 1) if lev == 0 else nx + side * (nc - 1)

    def across(at, scale, own, beyond, factor):
        t = 2.0 * scale / (own + jnp.exp(-beyond))
        if at is not None:
            t = jnp.where(at, t, 0.0)
        return t if factor is None else t * factor

    arrive(0, 3)
    for slot, side, factor in sides("gz"):
        where = tile(side, nz, LANES)
        for i in range(nl):
            k, scale, _ = level(i)
            t = across(beside(lane_b, side, LANES, k), scale, inv_k[i, :, where],
                       side_z(0, side, i), factor)
            b_z[slot, i] = t
            held[i, :, where] += t
    arrive(0, 2)
    for slot, side, factor in sides("gy"):
        where = tile(side, ny, ROWS)
        for i in range(nl):
            k, scale, _ = level(i)
            t = across(beside(row_b, side, ROWS, k), scale, inv_k[i, where, :],
                       side_y(0, side, i), factor)
            b_y[slot, i] = t
            held[i, where, :] += t

    def begin(i):
        inverse = 1.0 / (inv_d[i] + held[i])
        inv_d[i] = inverse
        dirs[1, i] = res[i] * inverse * inv_theta

    for i in range(1, nx - 1):
        begin(i)
    for lev in (0, 1):
        arrive(0, lev)
        for slot, side, factor in sides("gx"):
            i = edge(lev, side)
            t = across(None, (1.0, 2.0)[lev], inv_k[i], side_x(0, side, lev), factor)
            b_x[lev, slot] = t
            held[i] += t
        if lev == 0:
            for i in dict.fromkeys((0, nx - 1)):
                begin(i)
            start(1, 0)
    for i in range(nx, nl):
        begin(i)
    send_coarse(1)
    send_rows(1)
    start(1, 3)

    for turn in range(1, DEGREE + 1):
        rho_next = 1.0 / (2.0 * sigma - rho)
        keep = rho_next * rho
        gain = 2.0 * rho_next / delta
        rho = rho_next
        later = field(turn + 1)
        for kind in (0, 1, 2, 3):
            drain(turn - 1, kind)
        flow_x = None
        for i in range(nl):
            k = level(i)[0]
            d = dirs[turn, i]
            sol[i] = d if turn == 1 else sol[i] + d
            flow_y = t_y[i] * (d - roll(d, -k, 0))
            flow_z = t_z[i] * (d - roll(d, -k, 1))
            r = res[i] - held[i] * d
            r = r - (flow_y - roll(flow_y, k, 0)) - (flow_z - roll(flow_z, k, 1))
            if i not in (0, nx):
                r = r + flow_x
            if i not in (nx - 1, nl - 1):
                flow_x = t_x[i] * (d - dirs[turn, i + 1])
                r = r - flow_x
            res[i] = r
            later[i] = keep * d + gain * (r * inv_d[i])

        def add(at, t, wide):
            if turn < DEGREE:
                res[at] += t
            later[at] += wide * (t * inv_d[at])

        arrive(turn, 3)
        for slot, side, _ in sides("gz"):
            for i in range(nl):
                add((i, slice(None), tile(side, nz, LANES)),
                    b_z[slot, i] * side_z(turn, side, i), gain[:, :LANES])
        arrive(turn, 2)
        for slot, side, _ in sides("gy"):
            for i in range(nl):
                add((i, tile(side, ny, ROWS), slice(None)),
                    b_y[slot, i] * side_y(turn, side, i), gain)
        for lev in (0, 1):
            arrive(turn, lev)
            for slot, side, _ in sides("gx"):
                add((edge(lev, side),), b_x[lev, slot] * side_x(turn, side, lev), gain)
            if lev == 0 and turn < DEGREE:
                start(turn + 1, 0)
        if turn < DEGREE:
            send_coarse(turn + 1)
            send_rows(turn + 1)
            start(turn + 1, 3)

    for kind in (0, 1, 2, 3):
        drain(DEGREE, kind)


def shards(sizes, log_perm, source, low_bound, high_bound):
    nx, ny, nz = log_perm.shape
    nc = nx // 2
    nl = nx + nc
    pack = -(-nl // ROWS) * ROWS
    turns = DEGREE + 1
    f32 = lambda *shape: pltpu.VMEM(shape, jnp.float32)
    block = f32(nx, ny, nz)
    both = f32(nl, ny, nz)
    shape = jax.ShapeDtypeStruct((nl, ny, nz), jnp.float32)
    hbm = pl.BlockSpec(memory_space=pltpu.HBM)
    vmem = pl.BlockSpec(memory_space=pltpu.VMEM)
    sol, last = pl.pallas_call(
        functools.partial(kernel, sizes),
        out_shape=(shape, shape),
        in_specs=[hbm] * 4,
        out_specs=(vmem, vmem),
        scratch_shapes=[
            pltpu.SMEM((1,), jnp.float32),
            pltpu.SMEM((1,), jnp.float32),
            block, block,
            f32(turns, nl, ny, nz),
            f32(turns, 2, ny // 2, nz // 2),
            f32(turns, 2, pack, nz),
            f32(turns, 2, ny, nz),
            f32(turns, 2, ny // 2, nz // 2),
            f32(turns, 2, pack, nz),
            f32(turns, 2, nl, ny, LANES),
            both, both, both, both,
            f32(2, 2, ny, nz),
            f32(2, nl, ROWS, nz),
            f32(2, nl, ny, LANES),
            both, both, both,
            pltpu.SemaphoreType.DMA((4,)),
            pltpu.SemaphoreType.DMA((turns, 4, 2)),
            pltpu.SemaphoreType.DMA((turns, 4, 2)),
        ],
        compiler_params=pltpu.CompilerParams(
            collective_id=0, has_side_effects=True, vmem_limit_bytes=16 * 2**20),
    )(low_bound, high_bound, log_perm, source)
    total = sol + last
    fine = total[:nx]
    return fine, fine - jnp.repeat(total[nx:], 2, axis=0)


def solution(mesh):
    sizes = {axis: mesh.shape[axis] for axis in AXES}
    spec = P(("groups", "gx"), "gy", "gz")
    return jax.shard_map(
        functools.partial(shards, sizes),
        mesh=mesh,
        in_specs=(spec, spec, P(), P()),
        out_specs=(spec, spec),
        check_vma=False,
    )
```
